32 devices in a mesh: shot: 2 (over y), box: 8 (over z, x), sub: 2 (over core).
Axes of the slice: x: 2, y: 2, z: 4, core: 2. Of those that a mesh axis runs over, the one named last changes fastest.
Arguments:
- box_weights: float32 [64, 256, 128], P(('shot', 'box', 'sub')), parts along dimension 0, may hold values from -6 to 6
- velocity: float32 [8192], P('shot'), parts along dimension 0, may hold values from -4 to 4
- switch_kernel: float32 [128, 128], replicated, may hold values from -0.5 to 0.5
Outputs:
- final_weights: float32 [4, 4096, 128], P('shot', ('box', 'sub')), parts along dimension 0
The draws below stay inside these ranges and needn't reach their ends.
There are 2 independent parts, one for each index of `shot`. The reference program is written for one: setup_inputs(seed, part) draws one part's arguments, and reference() takes and returns one part's arrays. A program takes and returns all parts, laid end to end along the dimension named above; an argument that names none is the same for every part. Nothing has to cross between parts.
All inputs are finite; a program needn't handle non-finite values.
Results may differ from the reference program's by a relative error of at most 0.00013.
Values sent between devices are 32-bit elements; how exact they have to be, the bound alone decides.
No kernel may reach another device: no remote copies, remote signals or barrier semaphores. Data moves between devices by JAX's collectives and lax.ppermute only.
A program may use at most 64 MiB of HBM per device.

```python
import jax
import jax.numpy as jnp
from jax import lax

CHEB = 8
SRC_DEV = 2
TGT = 256
LEVELS = 4
SOURCES = 32
TARGETS = 4096


def level_of(stream_key, shape, split, least, high):
    factor_of, own = 1.0, jax.random.fold_in(stream_key, 6)
    for position, blocks in split:
        heights = jnp.exp(jax.random.uniform(jax.random.fold_in(own, position), (blocks,), jnp.float32, least / len(split), high / len(split)))
        factor_of = factor_of * jnp.repeat(heights, shape[position] // blocks).reshape([-1 if axis == position else 1 for axis in range(len(shape))])
    return factor_of


def scatter_about(stream_key, extent, scale, limit, split=(), held_as=jnp.bfloat16):
    result = jax.random.normal(stream_key, extent, jnp.float32) * scale
    if len(split) > 0:
        result = level_of(stream_key, extent, split, -0.22, 0.18) * result
    return jnp.clip(result, min=-limit, max=limit).astype(held_as)


def setup_inputs(seed: int = 0, part: int = 0) -> dict:
    streams_of = jax.random.split(jax.random.key(seed), 4)
    part_keys = jax.random.split(jax.random.fold_in(streams_of[3], part), 4)
    box_weights = scatter_about(part_keys[0], (SOURCES, TGT, 2 * CHEB * CHEB), 1.0, 6.0, ((0, 16),), jnp.float32)
    velocity = jnp.clip(jax.random.uniform(part_keys[1], (TARGETS,), jnp.float32, -4.0, 4.0), -4.0, 4.0)
    switch_kernel = scatter_about(streams_of[2], (2 * CHEB * CHEB, 2 * CHEB * CHEB), (2 * CHEB * CHEB) ** -0.5, 0.5, (), jnp.float32)
    return {"box_weights": box_weights, "velocity": velocity, "switch_kernel": switch_kernel}


half_root = 0.7071067811865476


def cheb_nodes():
    counter = jnp.arange(CHEB, dtype=jnp.float32)
    return jnp.cos(jnp.pi * (2.0 * counter + 1.0) / (2.0 * CHEB))


def lagrange_rows(points, node_values):
    differences = points[:, None] - node_values[None, :]
    node_gaps = node_values[:, None] - node_values[None, :]
    identity = jnp.eye(CHEB, dtype=jnp.float32)
    numerator = jnp.prod(jnp.where(identity[None, :, :] > 0.5, 1.0, differences[:, None, :]), axis=2)
    denominator = jnp.prod(jnp.where(identity > 0.5, 1.0, node_gaps), axis=1)
    return numerator / denominator[None, :]


def spread_coord(values, axis_dim):
    if axis_dim == 0:
        return jnp.repeat(values, CHEB)
    return jnp.tile(values, CHEB)


def level_tables(axis_dim):
    node_values = cheb_nodes()
    identity = jnp.eye(CHEB, dtype=jnp.float32)
    pair_eye = jnp.eye(2, dtype=jnp.float32)
    matrices = []
    coords = []
    for child_idx in (0, 1):
        child_pts = (node_values + (2.0 * child_idx - 1.0)) * 0.5
        lagrange = lagrange_rows(child_pts, node_values)
        if axis_dim == 0:
            single = jnp.kron(lagrange, identity)
        else:
            single = jnp.kron(identity, lagrange)
        matrices.append(jnp.kron(pair_eye, single))
        coords.append(spread_coord(child_pts, axis_dim))
    return jnp.concatenate(matrices, 0), jnp.stack(coords), spread_coord(node_values, axis_dim)


def rotate(values, angles):
    real_part = values[..., :CHEB * CHEB]
    imag_part = values[..., CHEB * CHEB:]
    cosines = jnp.cos(angles)
    sine_vals = jnp.sin(angles)
    return jnp.concatenate([real_part * cosines - imag_part * sine_vals, real_part * sine_vals + imag_part * cosines], -1)


def merge_blocks(blocks, omegas, weights, coord_in, coord_out):
    phase = omegas[None, None, :, :, None]
    first_term = rotate(blocks[:, 0][:, :, None], -phase * coord_in[0])
    second_term = rotate(blocks[:, 1][:, :, None], -phase * coord_in[1])
    joined = jnp.concatenate([first_term, second_term], -1)
    mixture = jnp.dot(joined.reshape(-1, 4 * CHEB * CHEB), weights, precision=lax.Precision.HIGHEST, preferred_element_type=jnp.float32)
    mixture = mixture.reshape(first_term.shape)
    return rotate(mixture, phase * coord_out) * half_root


def reference(box_weights, velocity, switch_kernel):
    current = box_weights
    vec_len = 2 * CHEB * CHEB
    for level_idx in range(LEVELS):
        weights, coord_in, coord_out = level_tables(level_idx % 2)
        src_count = current.shape[0]
        tgt_count = current.shape[1]
        omegas = velocity[:2 * tgt_count].reshape(2, tgt_count)
        groups = current.reshape(src_count // (2 * SRC_DEV), 1, 2, SRC_DEV, tgt_count, vec_len)

        def merge_one(group):
            return merge_blocks(group, omegas, weights, coord_in, coord_out)

        merged = lax.map(merge_one, groups)
        current = merged.reshape(src_count // 2, 2 * tgt_count, vec_len)
        if level_idx == LEVELS // 2 - 1:
            flat = jnp.dot(current.reshape(-1, vec_len), switch_kernel, precision=lax.Precision.HIGHEST, preferred_element_type=jnp.float32)
            current = flat.reshape(current.shape)
    return current
```

```python
import functools

import jax
import jax.numpy as jnp
import numpy as np
from jax import lax
from jax.experimental import pallas as pl
from jax.experimental.pallas import tpu as pltpu
from jax.sharding import PartitionSpec as P

CHEB = 8
POINTS = CHEB * CHEB
VEC = 2 * POINTS
HALF_ROOT = 0.7071067811865476
CHUNKS = 4
LANES = 128
VMEM_ROOM = 8 << 20


COS_SERIES = [1.0 / 87178291200.0 * -1.0, 1.0 / 479001600.0, -1.0 / 3628800.0, 1.0 / 40320.0, -1.0 / 720.0, 1.0 / 24.0, -0.5, 1.0]
SIN_SERIES = [-1.0 / 1307674368000.0, 1.0 / 6227020800.0, -1.0 / 39916800.0, 1.0 / 362880.0, -1.0 / 5040.0, 1.0 / 120.0, -1.0 / 6.0, 1.0]


def nodes():
    return np.cos(np.pi * (2.0 * np.arange(CHEB) + 1.0) / (2.0 * CHEB))


def child_matrices(axis_dim):
    z = nodes()
    found = []
    for child in (0, 1):
        y = (z + (2.0 * child - 1.0)) * 0.5
        rows = np.ones((CHEB, CHEB))
        for k in range(CHEB):
            for other in range(CHEB):
                if other != k:
                    rows[:, k] *= (y - z[other]) / (z[k] - z[other])
        single = np.kron(rows, np.eye(CHEB)) if axis_dim == 0 else np.kron(np.eye(CHEB), rows)
        found.append(np.kron(np.eye(2), single))
    return np.stack(found).astype(np.float32)


def lane_coefs(axis_dim):
    z = nodes()
    spread = np.repeat(z, CHEB) if axis_dim == 0 else np.tile(z, CHEB)
    sign = np.concatenate([-np.ones(POINTS), np.ones(POINTS)])
    table = np.zeros((8, VEC), np.float32)
    table[0] = 0.5 * np.concatenate([spread, spread]) * sign
    table[1] = 0.5 * sign
    return table


def cos_sin(angle):
    square = angle * angle
    c = jnp.full_like(square, COS_SERIES[0])
    for term in COS_SERIES[1:]:
        c = c * square + term
    s = jnp.full_like(square, SIN_SERIES[0])
    for term in SIN_SERIES[1:]:
        s = s * square + term
    return c, s * angle


def place(box_axis, sub_axis, sub_count):
    return lax.axis_index(box_axis) * sub_count + lax.axis_index(sub_axis)


def table_kernel(level, sub_count, tgt, vel_ref, coef_ref, out_ref):
    device = place("box", "sub", sub_count)
    code = lax.rem(device, 2 ** (level + 1))
    child = lax.rem(device // 2**level, 2)
    k = 2.0 * child.astype(jnp.float32) - 1.0
    rows = tgt // LANES
    for r in range(rows):
        row = vel_ref[pl.ds(code * rows + r, 1), :]
        omega = jnp.transpose(jnp.broadcast_to(row, (LANES, LANES)))
        c1, s1 = cos_sin(omega * coef_ref[0:1, :])
        ca, sa = cos_sin(omega * coef_ref[1:2, :])
        sa = sa * k
        p, q, u, t = c1 * ca, s1 * sa, s1 * ca, c1 * sa
        at = slice(r * LANES, (r + 1) * LANES)
        out_ref[0, at, :] = p - q
        out_ref[1, at, :] = -(u + t)
        out_ref[2, at, :] = p + q
        out_ref[3, at, :] = t - u
        out_ref[4, at, :] = (1.0 - 2.0 * s1 * s1) * HALF_ROOT
        out_ref[5, at, :] = (2.0 * HALF_ROOT) * s1 * c1


def tables(level, sub_count, tgt, vel, coefs):
    return pl.pallas_call(
        functools.partial(table_kernel, level, sub_count, tgt),
        out_shape=jax.ShapeDtypeStruct((6, tgt, VEC), jnp.float32),
        compiler_params=pltpu.CompilerParams(vmem_limit_bytes=VMEM_ROOM),
        name=f"tables{level}",
    )(vel, coefs)


def dot(a, b):
    return jnp.dot(a, b, precision=lax.Precision.HIGHEST, preferred_element_type=jnp.float32)


def turn(v, c, s):
    return v * c[None] + pltpu.roll(v, POINTS, 2) * s[None]


def own_kernel(level, sub_count, start, cur_ref, tab_ref, mat_ref, out_ref):
    at = slice(start, start + cur_ref.shape[1])
    child = lax.rem(place("box", "sub", sub_count) // 2**level, 2)
    turned = turn(cur_ref[...], tab_ref[0, at], tab_ref[1, at])
    out_ref[...] = dot(turned.reshape(-1, VEC), mat_ref[child]).reshape(out_ref.shape)


def far_kernel(level, sub_count, start, switch, *refs):
    own_ref, far_ref, tab_ref, mat_ref = refs[:4]
    outs = refs[5:] if switch else refs[4:]
    child = lax.rem(place("box", "sub", sub_count) // 2**level, 2)
    src, count, _ = far_ref.shape
    at = slice(start, start + count)
    turned = turn(far_ref[...], tab_ref[2, at], tab_ref[3, at])
    mixed = own_ref[...] + dot(turned.reshape(-1, VEC), mat_ref[1 - child]).reshape(far_ref.shape)
    result = turn(mixed, tab_ref[4, at], tab_ref[5, at])
    if switch:
        result = dot(result.reshape(-1, VEC), refs[4][...]).reshape(far_ref.shape)
    width = count // len(outs)
    for i, out in enumerate(outs):
        out[...] = result[:, i * width : (i + 1) * width]


def own_part(level, sub_count, cur, tab, mat, start):
    return pl.pallas_call(
        functools.partial(own_kernel, level, sub_count, start),
        out_shape=jax.ShapeDtypeStruct(cur.shape, jnp.float32),
        compiler_params=pltpu.CompilerParams(vmem_limit_bytes=VMEM_ROOM),
        name=f"own{level}",
    )(cur, tab, mat)


def far_part(level, sub_count, own, far, tab, mat, start, switch, pieces):
    src, count, _ = far.shape
    args = [own, far, tab, mat] + ([switch] if switch is not None else [])
    outs = pl.pallas_call(
        functools.partial(far_kernel, level, sub_count, start, switch is not None),
        out_shape=[jax.ShapeDtypeStruct((src, count // pieces, VEC), jnp.float32)] * pieces,
        compiler_params=pltpu.CompilerParams(vmem_limit_bytes=VMEM_ROOM),
        name=f"far{level}",
    )(*args)
    return outs


def swapped(value, axis, apart):
    mask = 2**apart
    pairs = [(source, source ^ mask) for source in range(lax.axis_size(axis))]
    return lax.ppermute(value, axis, pairs)


def body(box_weights, velocity, switch_kernel):
    sub_count = lax.axis_size("sub")
    sub_bits = sub_count.bit_length() - 1
    box_bits = lax.axis_size("box").bit_length() - 1
    levels = box_bits + sub_bits
    src, tgt, _ = box_weights.shape
    chunks = CHUNKS
    width = tgt // chunks
    vel = velocity.reshape(-1, LANES)
    mats = [jnp.asarray(child_matrices(e)) for e in (0, 1)]
    coefs = [jnp.asarray(lane_coefs(e)) for e in (0, 1)]
    tabs = [tables(m, sub_count, tgt, vel, coefs[m % 2]) for m in range(levels)]
    parts = [box_weights]
    starts = [0]
    for level in range(levels):
        axis, bit = ("sub", level) if level < sub_bits else ("box", level - sub_bits)
        switch = switch_kernel if level == levels // 2 - 1 else None
        pieces = chunks if level == 0 else 1
        new = []
        for part, start in zip(parts, starts):
            far = swapped(part, axis, bit)
            own = own_part(level, sub_count, part, tabs[level], mats[level % 2], start)
            new.extend(far_part(level, sub_count, own, far, tabs[level], mats[level % 2], start, switch, pieces))
        parts = new
        if level == 0:
            starts = [i * width for i in range(chunks)]
    return jnp.concatenate(parts, axis=1)


def solution(mesh):
    return jax.shard_map(
        body,
        mesh=mesh,
        in_specs=(P(("shot", "box", "sub"), None, None), P("shot"), P()),
        out_specs=P("shot", ("box", "sub"), None),
        check_vma=False,
    )
```

```python
import functools

import jax
import jax.numpy as jnp
import numpy as np
from jax import lax
from jax.experimental import pallas as pl
from jax.experimental.pallas import tpu as pltpu
from jax.sharding import PartitionSpec as P

CHEB = 8
POINTS = CHEB * CHEB
VEC = 2 * POINTS
HALF_ROOT = 0.7071067811865476
SHARES = (4, 4, 4, 4)
CHUNKS = len(SHARES)
SLOPE = 4
LANES = 128
KINDS = 6
VMEM_ROOM = 8 << 20


COS_SERIES = [-1.0 / 87178291200.0, 1.0 / 479001600.0, -1.0 / 3628800.0, 1.0 / 40320.0, -1.0 / 720.0, 1.0 / 24.0, -0.5, 1.0]
SIN_SERIES = [-1.0 / 1307674368000.0, 1.0 / 6227020800.0, -1.0 / 39916800.0, 1.0 / 362880.0, -1.0 / 5040.0, 1.0 / 120.0, -1.0 / 6.0, 1.0]


def nodes():
    return np.cos(np.pi * (2.0 * np.arange(CHEB) + 1.0) / (2.0 * CHEB))


def child_matrices(axis_dim):
    z = nodes()
    found = []
    for child in (0, 1):
        y = (z + (2.0 * child - 1.0)) * 0.5
        rows = np.ones((CHEB, CHEB))
        for k in range(CHEB):
            for other in range(CHEB):
                if other != k:
                    rows[:, k] *= (y - z[other]) / (z[k] - z[other])
        single = np.kron(rows, np.eye(CHEB)) if axis_dim == 0 else np.kron(np.eye(CHEB), rows)
        found.append(np.kron(np.eye(2), single).astype(np.float32))
    both = np.stack([np.concatenate(found, 0), np.concatenate(found[::-1], 0)])
    high = both.astype(jnp.bfloat16)
    low = (both - high.astype(np.float32)).astype(jnp.bfloat16)
    return np.concatenate([high, low], -1)


def cos_sin(angle):
    square = angle * angle
    c = jnp.full_like(square, COS_SERIES[0])
    for term in COS_SERIES[1:]:
        c = c * square + term
    s = jnp.full_like(square, SIN_SERIES[0])
    for term in SIN_SERIES[1:]:
        s = s * square + term
    return c, s * angle


def halves(x):
    high = x.astype(jnp.bfloat16)
    return high, (x - high.astype(jnp.float32)).astype(jnp.bfloat16)


def mm(a, b):
    return jnp.dot(a, b, preferred_element_type=jnp.float32)


def mixed_with(x, mat):
    high, low = halves(x)
    wide = mm(high, mat)
    n = wide.shape[1] // 2
    return wide[:, :n] + wide[:, n:] + mm(low, mat[:, :n])


def expand(values, spots):
    a = values.astype(jnp.bfloat16)
    rest = values - a.astype(jnp.float32)
    b = rest.astype(jnp.bfloat16)
    c = (rest - b.astype(jnp.float32)).astype(jnp.bfloat16)
    pieces = jnp.concatenate([a.astype(jnp.float32), b.astype(jnp.float32), c.astype(jnp.float32)], 0)
    return lax.dot_general(
        pieces.astype(jnp.bfloat16), spots, (((0,), (0,)), ((), ())), preferred_element_type=jnp.float32
    )


def prologue_kernel(levels, sub_count, x_hbm, vel_hbm, even_hbm, odd_hbm, sw_hbm, x_ref, even_ref, odd_ref, sw_ref, tab_ref, vel_ref, sw_in, sems):
    copies = [
        pltpu.make_async_copy(vel_hbm, vel_ref, sems.at[0]),
        pltpu.make_async_copy(x_hbm, x_ref, sems.at[1]),
        pltpu.make_async_copy(even_hbm, even_ref, sems.at[2]),
        pltpu.make_async_copy(odd_hbm, odd_ref, sems.at[3]),
        pltpu.make_async_copy(sw_hbm, sw_in, sems.at[4]),
    ]
    for copy in copies:
        copy.start()
    device = lax.axis_index("box") * sub_count + lax.axis_index("sub")
    tgt = tab_ref.shape[2]
    rows = tgt // LANES
    node = lax.broadcasted_iota(jnp.int32, (CHEB, LANES), 0)
    z = jnp.zeros((CHEB, LANES), jnp.float32)
    for k, value in enumerate(nodes()):
        z = jnp.where(node == k, float(value), z)
    node = lax.broadcasted_iota(jnp.int32, (3 * CHEB, VEC), 0) % CHEB
    lane = lax.broadcasted_iota(jnp.int32, (3 * CHEB, VEC), 1)
    sign = jnp.where(lane < POINTS, -1.0, 1.0)
    point = lane % POINTS
    spots = []
    for spot in (point // CHEB, point % CHEB):
        hit = jnp.where(spot == node, 1.0, 0.0)
        spots.append((hit.astype(jnp.bfloat16), (hit * sign).astype(jnp.bfloat16)))
    copies[0].wait()
    for level in range(levels):
        code = device % 2 ** (level + 1)
        child = (device // 2**level) % 2
        k = 2.0 * child.astype(jnp.float32) - 1.0
        plain, signed = spots[level % 2]
        for r in range(rows):
            half = 0.5 * jnp.broadcast_to(vel_ref[pl.ds(code * rows + r, 1), :], (CHEB, LANES))
            c1, s1 = cos_sin(half * z)
            ca, sa = cos_sin(half)
            sa = sa * k
            p, q, u, t = c1 * ca, s1 * sa, s1 * ca, c1 * sa
            cosines = (p - q, p + q, (1.0 - 2.0 * s1 * s1) * HALF_ROOT)
            sines = (-(u + t), t - u, (2.0 * HALF_ROOT) * s1 * c1)
            at = slice(r * LANES, (r + 1) * LANES)
            wide = expand(jnp.concatenate(cosines, 1), plain)
            wide_s = expand(jnp.concatenate(sines, 1), signed)
            for i in range(3):
                tab_ref[level, 2 * i, at, :] = wide[i * LANES : (i + 1) * LANES]
                tab_ref[level, 2 * i + 1, at, :] = wide_s[i * LANES : (i + 1) * LANES]
    copies[4].wait()
    high, low = halves(sw_in[...])
    sw_ref[...] = jnp.concatenate([high, low], 1)
    for copy in copies[1:4]:
        copy.wait()


def prologue(levels, sub_count, x, vel, switch):
    tgt = x.shape[1]
    mats = [jnp.asarray(child_matrices(e)) for e in (0, 1)]
    anywhere = pl.BlockSpec(memory_space=pltpu.HBM)
    vmem = pl.BlockSpec(memory_space=pltpu.VMEM)
    return pl.pallas_call(
        functools.partial(prologue_kernel, levels, sub_count),
        out_shape=[
            jax.ShapeDtypeStruct(x.shape, jnp.float32),
            jax.ShapeDtypeStruct(mats[0].shape, jnp.bfloat16),
            jax.ShapeDtypeStruct(mats[1].shape, jnp.bfloat16),
            jax.ShapeDtypeStruct((VEC, 2 * VEC), jnp.bfloat16),
            jax.ShapeDtypeStruct((levels, KINDS, tgt, VEC), jnp.float32),
        ],
        in_specs=[anywhere] * 5,
        out_specs=[vmem] * 5,
        scratch_shapes=[
            pltpu.VMEM(vel.shape, jnp.float32),
            pltpu.VMEM(switch.shape, jnp.float32),
            pltpu.SemaphoreType.DMA((5,)),
        ],
        compiler_params=pltpu.CompilerParams(vmem_limit_bytes=VMEM_ROOM),
        name="prologue",
    )(*[pltpu.with_memory_space_constraint(v, pltpu.HBM) for v in (x, vel, mats[0], mats[1], switch)])


def turn(v, c, s):
    return v * c[None] + pltpu.roll(v, POINTS, 2) * s[None]


def level_value(level, sub_count, start, own_ref, far_ref, tab_ref, mat_ref, sw_ref):
    child = ((lax.axis_index("box") * sub_count + lax.axis_index("sub")) // 2**level) % 2
    shape = far_ref.shape
    at = slice(start, start + shape[1])
    own = turn(own_ref[...], tab_ref[level, 0, at], tab_ref[level, 1, at])
    far = turn(far_ref[...], tab_ref[level, 2, at], tab_ref[level, 3, at])
    both = jnp.concatenate([own.reshape(-1, VEC), far.reshape(-1, VEC)], 1)
    mixed = mixed_with(both, mat_ref[child]).reshape(shape)
    result = turn(mixed, tab_ref[level, 4, at], tab_ref[level, 5, at])
    if sw_ref is not None:
        result = mixed_with(result.reshape(-1, VEC), sw_ref[...]).reshape(shape)
    return result


def level_kernel(level, sub_count, start, switched, n_in, *refs):
    own_ref, far_ref, tab_ref, mat_ref = refs[:4]
    outs = refs[n_in:]
    result = level_value(level, sub_count, start, own_ref, far_ref, tab_ref, mat_ref, refs[4] if switched else None)
    at = 0
    for out in outs:
        out[...] = result[:, at : at + out.shape[1]]
        at += out.shape[1]


def level_part(level, sub_count, start, own, far, tab, mat, switch, widths, after):
    src = far.shape[0]
    args = [own, far, tab, mat] + ([switch] if switch is not None else [])
    specs = [pl.BlockSpec(memory_space=pltpu.VMEM)] * len(args)
    if after is not None:
        args.append(after)
        specs.append(pl.BlockSpec(memory_space=pl.ANY))
    return pl.pallas_call(
        functools.partial(level_kernel, level, sub_count, start, switch is not None, len(args)),
        out_shape=[jax.ShapeDtypeStruct((src, w, VEC), jnp.float32) for w in widths],
        in_specs=specs,
        out_specs=[pl.BlockSpec(memory_space=pltpu.VMEM)] * len(widths),
        compiler_params=pltpu.CompilerParams(vmem_limit_bytes=VMEM_ROOM),
        name=f"level{level}_{start}",
    )(*args)


def last_kernel(level, sub_count, start, switched, n_done, n_in, *refs):
    own_ref, far_ref, tab_ref, mat_ref = refs[:4]
    dones = refs[n_in - n_done : n_in]
    out_hbm, held, sems = refs[n_in:]
    copies = []
    at = 0
    for i, done in enumerate(dones):
        copies.append(pltpu.make_async_copy(done, out_hbm.at[:, pl.ds(at, done.shape[1])], sems.at[i]))
        at += done.shape[1]
    for copy in copies:
        copy.start()
    held[...] = level_value(level, sub_count, start, own_ref, far_ref, tab_ref, mat_ref, refs[4] if switched else None)
    mine = pltpu.make_async_copy(held, out_hbm.at[:, pl.ds(start, held.shape[1])], sems.at[n_done])
    mine.start()
    for copy in copies:
        copy.wait()
    mine.wait()


def last_part(level, sub_count, start, own, far, tab, mat, switch, dones, tgt):
    args = [own, far, tab, mat] + ([switch] if switch is not None else []) + dones
    return pl.pallas_call(
        functools.partial(last_kernel, level, sub_count, start, switch is not None, len(dones), len(args)),
        out_shape=jax.ShapeDtypeStruct((far.shape[0], tgt, VEC), jnp.float32),
        in_specs=[pl.BlockSpec(memory_space=pltpu.VMEM)] * len(args),
        out_specs=pl.BlockSpec(memory_space=pltpu.HBM),
        scratch_shapes=[pltpu.VMEM(far.shape, jnp.float32), pltpu.SemaphoreType.DMA((len(dones) + 1,))],
        compiler_params=pltpu.CompilerParams(vmem_limit_bytes=VMEM_ROOM),
        name="last",
    )(*args)


def swapped(value, axis, apart):
    mask = 2**apart
    pairs = [(source, source ^ mask) for source in range(lax.axis_size(axis))]
    return lax.ppermute(value, axis, pairs)


def order_of(levels, chunks):
    steps = [(SLOPE * m + c, m, c) for m in range(1, levels) for c in range(chunks)]
    return [(m, c) for _, m, c in sorted(steps, key=lambda s: (s[0], -s[1]))]


def body(box_weights, velocity, switch_kernel):
    sub_count = lax.axis_size("sub")
    sub_bits = sub_count.bit_length() - 1
    levels = lax.axis_size("box").bit_length() - 1 + sub_bits
    src, tgt, _ = box_weights.shape
    widths = [tgt * n // 16 for n in SHARES]
    starts = [sum(widths[:c]) for c in range(CHUNKS)]

    def far_of(value, level):
        return swapped(value, "sub", level) if level < sub_bits else swapped(value, "box", level - sub_bits)

    far = far_of(box_weights, 0)
    x, even, odd, sw, tab = prologue(levels, sub_count, box_weights, velocity.reshape(-1, LANES), switch_kernel)
    mats = (even, odd)

    def switch_at(level):
        return sw if level == levels // 2 - 1 else None

    parts = list(level_part(0, sub_count, 0, x, far, tab, mats[0], switch_at(0), widths, None))
    fars = [far_of(part, 1) for part in parts]
    after = None
    for level, c in order_of(levels, CHUNKS)[:-1]:
        args = (level, sub_count, starts[c], parts[c], fars[c], tab, mats[level % 2], switch_at(level))
        (parts[c],) = level_part(*args, [widths[c]], after)
        after = parts[c]
        if level < levels - 1:
            fars[c] = far_of(parts[c], level + 1)
    last = levels - 1
    return last_part(last, sub_count, starts[-1], parts[-1], fars[-1], tab, mats[last % 2], switch_at(last), parts[:-1], tgt)


def solution(mesh):
    return jax.shard_map(
        body,
        mesh=mesh,
        in_specs=(P(("shot", "box", "sub"), None, None), P("shot"), P()),
        out_specs=P("shot", ("box", "sub"), None),
        check_vma=False,
    )
```

```python
import functools

import jax
import jax.numpy as jnp
import numpy as np
from jax import lax
from jax.experimental import pallas as pl
from jax.experimental.pallas import tpu as pltpu
from jax.sharding import PartitionSpec as P


CHEB = 8
POINTS = CHEB * CHEB
VEC = 2 * POINTS
HALF_ROOT = 0.7071067811865476
SHARES = (8, 4, 4)
EARLY = (False, False, True)
LANES = 128
KINDS = 6
VMEM_ROOM = 8 << 20


COS_SERIES = [-1.0 / 87178291200.0, 1.0 / 479001600.0, -1.0 / 3628800.0, 1.0 / 40320.0, -1.0 / 720.0, 1.0 / 24.0, -0.5, 1.0]
SIN_SERIES = [-1.0 / 1307674368000.0, 1.0 / 6227020800.0, -1.0 / 39916800.0, 1.0 / 362880.0, -1.0 / 5040.0, 1.0 / 120.0, -1.0 / 6.0, 1.0]


def nodes():
    return np.cos(np.pi * (2.0 * np.arange(CHEB) + 1.0) / (2.0 * CHEB))


def child_matrices(axis_dim):
    z = nodes()
    found = []
    for child in (0, 1):
        y = (z + (2.0 * child - 1.0)) * 0.5
        rows = np.ones((CHEB, CHEB))
        for k in range(CHEB):
            for other in range(CHEB):
                if other != k:
                    rows[:, k] *= (y - z[other]) / (z[k] - z[other])
        single = np.kron(rows, np.eye(CHEB)) if axis_dim == 0 else np.kron(np.eye(CHEB), rows)
        found.append(np.kron(np.eye(2), single).astype(np.float32))
    both = np.stack([np.concatenate(found, 0), np.concatenate(found[::-1], 0)])
    high = both.astype(jnp.bfloat16)
    low = (both - high.astype(np.float32)).astype(jnp.bfloat16)
    return np.concatenate([high, low], -1)


def cos_sin(angle):
    square = angle * angle
    c = jnp.full_like(square, COS_SERIES[0])
    for term in COS_SERIES[1:]:
        c = c * square + term
    s = jnp.full_like(square, SIN_SERIES[0])
    for term in SIN_SERIES[1:]:
        s = s * square + term
    return c, s * angle


def halves(x):
    high = x.astype(jnp.bfloat16)
    return high, (x - high.astype(jnp.float32)).astype(jnp.bfloat16)


def mm(a, b):
    return jnp.dot(a, b, preferred_element_type=jnp.float32)


def mixed_with(x, mat):
    high, low = halves(x)
    wide = mm(high, mat)
    n = wide.shape[1] // 2
    return wide[:, :n] + wide[:, n:] + mm(low, mat[:, :n])


def expand(values, spots):
    a = values.astype(jnp.bfloat16)
    rest = values - a.astype(jnp.float32)
    b = rest.astype(jnp.bfloat16)
    c = (rest - b.astype(jnp.float32)).astype(jnp.bfloat16)
    pieces = jnp.concatenate([a.astype(jnp.float32), b.astype(jnp.float32), c.astype(jnp.float32)], 0)
    return lax.dot_general(
        pieces.astype(jnp.bfloat16), spots, (((0,), (0,)), ((), ())), preferred_element_type=jnp.float32
    )


def prologue_kernel(levels, sub_count, x_hbm, vel_hbm, even_hbm, odd_hbm, sw_hbm, x_ref, even_ref, odd_ref, sw_ref, tab_ref, vel_ref, sw_in, sems):
    copies = [
        pltpu.make_async_copy(vel_hbm, vel_ref, sems.at[0]),
        pltpu.make_async_copy(x_hbm, x_ref, sems.at[1]),
        pltpu.make_async_copy(even_hbm, even_ref, sems.at[2]),
        pltpu.make_async_copy(odd_hbm, odd_ref, sems.at[3]),
        pltpu.make_async_copy(sw_hbm, sw_in, sems.at[4]),
    ]
    for copy in copies:
        copy.start()
    device = lax.axis_index("box") * sub_count + lax.axis_index("sub")
    tgt = tab_ref.shape[2]
    rows = tgt // LANES
    node = lax.broadcasted_iota(jnp.int32, (CHEB, LANES), 0)
    z = jnp.zeros((CHEB, LANES), jnp.float32)
    for k, value in enumerate(nodes()):
        z = jnp.where(node == k, float(value), z)
    node = lax.broadcasted_iota(jnp.int32, (3 * CHEB, VEC), 0) % CHEB
    lane = lax.broadcasted_iota(jnp.int32, (3 * CHEB, VEC), 1)
    sign = jnp.where(lane < POINTS, -1.0, 1.0)
    point = lane % POINTS
    spots = []
    for spot in (point // CHEB, point % CHEB):
        hit = jnp.where(spot == node, 1.0, 0.0)
        spots.append((hit.astype(jnp.bfloat16), (hit * sign).astype(jnp.bfloat16)))
    copies[0].wait()
    for entry in range(levels + 1):
        level = min(entry, levels - 1)
        code = device % 2 ** (level + 1)
        child = (device // 2**level) % 2
        if entry == levels:
            code = code + (1 - 2 * child) * 2**level
        k = 2.0 * child.astype(jnp.float32) - 1.0
        plain, signed = spots[level % 2]
        for r in range(rows):
            half = 0.5 * jnp.broadcast_to(vel_ref[pl.ds(code * rows + r, 1), :], (CHEB, LANES))
            c1, s1 = cos_sin(half * z)
            ca, sa = cos_sin(half)
            sa = sa * k
            p, q, u, t = c1 * ca, s1 * sa, s1 * ca, c1 * sa
            cosines = (p - q, p + q, (1.0 - 2.0 * s1 * s1) * HALF_ROOT)
            sines = (-(u + t), t - u, (2.0 * HALF_ROOT) * s1 * c1)
            at = slice(r * LANES, (r + 1) * LANES)
            wide = expand(jnp.concatenate(cosines, 1), plain)
            wide_s = expand(jnp.concatenate(sines, 1), signed)
            for i in range(3):
                tab_ref[entry, 2 * i, at, :] = wide[i * LANES : (i + 1) * LANES]
                tab_ref[entry, 2 * i + 1, at, :] = wide_s[i * LANES : (i + 1) * LANES]
    copies[4].wait()
    high, low = halves(sw_in[...])
    sw_ref[...] = jnp.concatenate([high, low], 1)
    for copy in copies[1:4]:
        copy.wait()


def prologue(levels, sub_count, x, vel, switch):
    tgt = x.shape[1]
    mats = [jnp.asarray(child_matrices(e)) for e in (0, 1)]
    anywhere = pl.BlockSpec(memory_space=pltpu.HBM)
    vmem = pl.BlockSpec(memory_space=pltpu.VMEM)
    return pl.pallas_call(
        functools.partial(prologue_kernel, levels, sub_count),
        out_shape=[
            jax.ShapeDtypeStruct(x.shape, jnp.float32),
            jax.ShapeDtypeStruct(mats[0].shape, jnp.bfloat16),
            jax.ShapeDtypeStruct(mats[1].shape, jnp.bfloat16),
            jax.ShapeDtypeStruct((VEC, 2 * VEC), jnp.bfloat16),
            jax.ShapeDtypeStruct((levels + 1, KINDS, tgt, VEC), jnp.float32),
        ],
        in_specs=[anywhere] * 5,
        out_specs=[vmem] * 5,
        scratch_shapes=[
            pltpu.VMEM(vel.shape, jnp.float32),
            pltpu.VMEM(switch.shape, jnp.float32),
            pltpu.SemaphoreType.DMA((5,)),
        ],
        compiler_params=pltpu.CompilerParams(vmem_limit_bytes=VMEM_ROOM),
        name="prologue",
    )(*[pltpu.with_memory_space_constraint(v, pltpu.HBM) for v in (x, vel, mats[0], mats[1], switch)])


def turn(v, c, s):
    return v * c[None] + pltpu.roll(v, POINTS, 2) * s[None]


def bit_of(sub_count, level):
    return ((lax.axis_index("box") * sub_count + lax.axis_index("sub")) // 2**level) % 2


def merged(own, far, tab_ref, entry, start, mat):
    shape = far.shape
    at = slice(start, start + shape[1])
    own = turn(own, tab_ref[entry, 0, at], tab_ref[entry, 1, at])
    far = turn(far, tab_ref[entry, 2, at], tab_ref[entry, 3, at])
    both = jnp.concatenate([own.reshape(-1, VEC), far.reshape(-1, VEC)], 1)
    mixed = mixed_with(both, mat).reshape(shape)
    return turn(mixed, tab_ref[entry, 4, at], tab_ref[entry, 5, at])


def level_value(plan, level, start, own, far, tab_ref, mat_ref, sw_ref):
    result = merged(own, far, tab_ref, level, start, mat_ref[bit_of(plan.sub_count, level)])
    if level == plan.switch_level:
        result = mixed_with(result.reshape(-1, VEC), sw_ref[...]).reshape(result.shape)
    return result


def call(kernel, args, outs, scratch=(), specs=None, out_specs=None, aliases=None):
    specs = list(specs or [VMEM_SPEC] * len(args))
    return pl.pallas_call(
        kernel,
        out_shape=[jax.ShapeDtypeStruct(s, jnp.float32) for s in outs],
        in_specs=specs,
        out_specs=out_specs or [VMEM_SPEC] * len(outs),
        scratch_shapes=list(scratch),
        input_output_aliases=aliases or {},
        compiler_params=pltpu.CompilerParams(vmem_limit_bytes=VMEM_ROOM),
    )(*args)


VMEM_SPEC = pl.BlockSpec(memory_space=pltpu.VMEM)
HBM_SPEC = pl.BlockSpec(memory_space=pltpu.HBM)


class Plan:
    def __init__(self, sub_count, levels, shape):
        self.sub_count = sub_count
        self.sub_bits = sub_count.bit_length() - 1
        self.levels = levels
        self.switch_level = levels // 2 - 1
        self.src, self.tgt, _ = shape
        total = sum(SHARES)
        self.widths = [self.tgt * n // total for n in SHARES]
        self.starts = [sum(self.widths[:c]) for c in range(len(SHARES))]

    def far_of(self, value, level):
        if level < self.sub_bits:
            return swapped(value, "sub", level)
        return swapped(value, "box", level - self.sub_bits)


def first_step(plan, x, far, tab, mat, sw):
    half = plan.src // 2

    def kernel(x_ref, far_ref, tab_ref, mat_ref, sw_ref, *outs):
        result = level_value(plan, 0, 0, x_ref[...], far_ref[...], tab_ref, mat_ref, sw_ref)
        upper = bit_of(plan.sub_count, plan.levels - 1) == 1
        outs = list(outs)
        for start, width, early in zip(plan.starts, plan.widths, EARLY):
            part = result[:, start : start + width]
            if early:
                outs.pop(0)[...] = jnp.where(upper, part[half:], part[:half])
                outs.pop(0)[...] = jnp.where(upper, part[:half], part[half:])
            else:
                outs.pop(0)[...] = part

    outs = []
    for width, early in zip(plan.widths, EARLY):
        outs += [(half, width, VEC)] * 2 if early else [(plan.src, width, VEC)]
    outs = list(call(kernel, [x, far, tab, mat, sw], outs))
    return [(outs.pop(0), outs.pop(0)) if early else (outs.pop(0),) for early in EARLY]


def step(plan, level, c, own, far, tab, mat, sw):
    def kernel(own_ref, far_ref, tab_ref, mat_ref, sw_ref, *rest):
        rest[-1][...] = level_value(plan, level, plan.starts[c], own_ref[...], far_ref[...], tab_ref, mat_ref, sw_ref)

    return call(kernel, [own, far, tab, mat, sw], [own.shape])[0]


def join(kept, received):
    def kernel(a_ref, b_ref, *rest):
        n = a_ref.shape[0]
        rest[-1][:n] = a_ref[...]
        rest[-1][n:] = b_ref[...]

    return call(kernel, [kept, received], [(2 * kept.shape[0], *kept.shape[1:])])[0]


def early_end(plan, c, own, far, tab, mats, sw):
    last = plan.levels - 1
    start = plan.starts[c]

    def kernel(own_ref, far_ref, tab_ref, mat_ref, last_mat_ref, sw_ref, mine_ref, theirs_ref):
        x = level_value(plan, last - 1, start, own_ref[...], far_ref[...], tab_ref, mat_ref, sw_ref)
        half = x.shape[0] // 2
        mat = last_mat_ref[bit_of(plan.sub_count, last)]
        theirs_ref[...] = merged(x[:half], x[half:], tab_ref, last + 1, start, mat)
        mine_ref[...] = merged(x[:half], x[half:], tab_ref, last, start, mat)

    shape = (own.shape[0] // 2, *own.shape[1:])
    return call(kernel, [own, far, tab, mats[(last - 1) % 2], mats[last % 2], sw], [shape, shape])


def finish(plan, results):
    flat = [part for result in results for part in result]

    def kernel(*refs):
        parts, out_hbm, sems = list(refs[: len(flat)]), refs[-2], refs[-1]
        upper = bit_of(plan.sub_count, plan.levels - 1)
        copies = []
        for start, result in zip(plan.starts, results):
            for i in range(len(result)):
                ref = parts.pop(0)
                rows, count, _ = ref.shape
                box = 0 if len(result) == 1 else (upper if i == 0 else 1 - upper) * rows
                place = out_hbm.at[pl.ds(box, rows), pl.ds(start, count)]
                copies.append(pltpu.make_async_copy(ref, place, sems.at[len(copies)]))
        for copy in copies:
            copy.start()
        for copy in copies:
            copy.wait()

    scratch = [pltpu.SemaphoreType.DMA((len(flat),))]
    return call(kernel, flat, [(plan.src, plan.tgt, VEC)], scratch, None, [HBM_SPEC])[0]


def swapped(value, axis, apart):
    mask = 2**apart
    pairs = [(source, source ^ mask) for source in range(lax.axis_size(axis))]
    return lax.ppermute(value, axis, pairs)


def levels_of(box_weights, velocity, switch_kernel):
    sub_count = lax.axis_size("sub")
    levels = lax.axis_size("box").bit_length() - 1 + sub_count.bit_length() - 1
    plan = Plan(sub_count, levels, box_weights.shape)
    last = levels - 1

    far = plan.far_of(box_weights, 0)
    x, even, odd, sw, tab = prologue(levels, sub_count, box_weights, velocity.reshape(-1, LANES), switch_kernel)
    mats = (even, odd)
    parts = first_step(plan, x, far, tab, mats[0], sw)
    results = []
    for c, (part, *leaving) in enumerate(parts):
        early = bool(leaving)
        if early:
            received = plan.far_of(leaving[0], last)
            part = join(part, received)
        for level in range(1, last - 1 if early else levels):
            far = plan.far_of(part, level)
            part = step(plan, level, c, part, far, tab, mats[level % 2], sw)
        if early:
            far = plan.far_of(part, last - 1)
            mine, theirs = early_end(plan, c, part, far, tab, mats, sw)
            results.append((mine, plan.far_of(theirs, last)))
        else:
            results.append((part,))
    return finish(plan, results)


def solution(mesh):
    return jax.shard_map(
        levels_of,
        mesh=mesh,
        in_specs=(P(("shot", "box", "sub"), None, None), P("shot"), P()),
        out_specs=P("shot", ("box", "sub"), None),
        check_vma=False,
    )
```

```python
import functools

import jax
import jax.numpy as jnp
import numpy as np
from jax import lax
from jax.experimental import pallas as pl
from jax.experimental.pallas import tpu as pltpu
from jax.sharding import PartitionSpec as P


CHEB = 8
POINTS = CHEB * CHEB
VEC = 2 * POINTS
HALF_ROOT = 0.7071067811865476
SHARES = (6, 5, 5)
PLAIN, SPLIT, DOUBLE = range(3)
KIND = (PLAIN, PLAIN, DOUBLE)
LANES = 128
ENTRIES = 6
VMEM_ROOM = 8 << 20


COS_SERIES = [-1.0 / 87178291200.0, 1.0 / 479001600.0, -1.0 / 3628800.0, 1.0 / 40320.0, -1.0 / 720.0, 1.0 / 24.0, -0.5, 1.0]
SIN_SERIES = [-1.0 / 1307674368000.0, 1.0 / 6227020800.0, -1.0 / 39916800.0, 1.0 / 362880.0, -1.0 / 5040.0, 1.0 / 120.0, -1.0 / 6.0, 1.0]


def nodes():
    return np.cos(np.pi * (2.0 * np.arange(CHEB) + 1.0) / (2.0 * CHEB))


def child_matrices(axis_dim):
    z = nodes()
    found = []
    for child in (0, 1):
        y = (z + (2.0 * child - 1.0)) * 0.5
        rows = np.ones((CHEB, CHEB))
        for k in range(CHEB):
            for other in range(CHEB):
                if other != k:
                    rows[:, k] *= (y - z[other]) / (z[k] - z[other])
        single = np.kron(rows, np.eye(CHEB)) if axis_dim == 0 else np.kron(np.eye(CHEB), rows)
        found.append(np.kron(np.eye(2), single).astype(np.float32))
    both = np.stack([np.concatenate(found, 0), np.concatenate(found[::-1], 0)])
    high = both.astype(jnp.bfloat16)
    low = (both - high.astype(np.float32)).astype(jnp.bfloat16)
    return np.concatenate([high, low], -1)


def cos_sin(angle):
    square = angle * angle
    c = jnp.full_like(square, COS_SERIES[0])
    for term in COS_SERIES[1:]:
        c = c * square + term
    s = jnp.full_like(square, SIN_SERIES[0])
    for term in SIN_SERIES[1:]:
        s = s * square + term
    return c, s * angle


def halves(x):
    high = x.astype(jnp.bfloat16)
    return high, (x - high.astype(jnp.float32)).astype(jnp.bfloat16)


def mm(a, b):
    return jnp.dot(a, b, preferred_element_type=jnp.float32)


def mixed_with(x, mat):
    high, low = halves(x)
    m, n = x.shape[0], mat.shape[1] // 2
    wide = mm(jnp.concatenate([high, low], 0), mat)
    return (wide[:m, :n] + wide[m:, :n]) + (wide[:m, n:] + wide[m:, n:])


def expand(values, spots):
    a = values.astype(jnp.bfloat16)
    rest = values - a.astype(jnp.float32)
    b = rest.astype(jnp.bfloat16)
    c = (rest - b.astype(jnp.float32)).astype(jnp.bfloat16)
    pieces = jnp.concatenate([a.astype(jnp.float32), b.astype(jnp.float32), c.astype(jnp.float32)], 0)
    return lax.dot_general(
        pieces.astype(jnp.bfloat16), spots, (((0,), (0,)), ((), ())), preferred_element_type=jnp.float32
    )


def prologue_kernel(levels, sub_count, x_hbm, vel_hbm, even_hbm, odd_hbm, sw_hbm, x_ref, even_ref, odd_ref, sw_ref, tab_ref, vel_ref, sw_in, sems):
    copies = [
        pltpu.make_async_copy(vel_hbm, vel_ref, sems.at[0]),
        pltpu.make_async_copy(x_hbm, x_ref, sems.at[1]),
        pltpu.make_async_copy(even_hbm, even_ref, sems.at[2]),
        pltpu.make_async_copy(odd_hbm, odd_ref, sems.at[3]),
        pltpu.make_async_copy(sw_hbm, sw_in, sems.at[4]),
    ]
    for copy in copies:
        copy.start()
    device = lax.axis_index("box") * sub_count + lax.axis_index("sub")
    tgt = tab_ref.shape[2]
    rows = tgt // LANES
    node = lax.broadcasted_iota(jnp.int32, (CHEB, LANES), 0)
    z = jnp.zeros((CHEB, LANES), jnp.float32)
    for k, value in enumerate(nodes()):
        z = jnp.where(node == k, float(value), z)
    node = lax.broadcasted_iota(jnp.int32, (3 * CHEB, VEC), 0) % CHEB
    lane = lax.broadcasted_iota(jnp.int32, (3 * CHEB, VEC), 1)
    sign = jnp.where(lane < POINTS, -1.0, 1.0)
    point = lane % POINTS
    spots = []
    for spot in (point // CHEB, point % CHEB):
        hit = jnp.where(spot == node, 1.0, 0.0)
        spots.append((hit.astype(jnp.bfloat16), (hit * sign).astype(jnp.bfloat16)))
    copies[0].wait()
    for entry in range(levels + 1):
        level = min(entry, levels - 1)
        code = device % 2 ** (level + 1)
        child = (device // 2**level) % 2
        if entry == levels:
            code = code + (1 - 2 * child) * 2**level
        k = 2.0 * child.astype(jnp.float32) - 1.0
        plain, signed = spots[level % 2]
        for r in range(rows):
            half = 0.5 * jnp.broadcast_to(vel_ref[pl.ds(code * rows + r, 1), :], (CHEB, LANES))
            c1, s1 = cos_sin(half * z)
            ca, sa = cos_sin(half)
            sa = sa * k
            p, q, u, t = c1 * ca, s1 * sa, s1 * ca, c1 * sa
            cosines = (p - q, p + q, (1.0 - 2.0 * s1 * s1) * HALF_ROOT)
            sines = (-(u + t), t - u, (2.0 * HALF_ROOT) * s1 * c1)
            at = slice(r * LANES, (r + 1) * LANES)
            wide = expand(jnp.concatenate(cosines, 1), plain)
            wide_s = expand(jnp.concatenate(sines, 1), signed)
            for i in range(3):
                tab_ref[entry, 2 * i, at, :] = wide[i * LANES : (i + 1) * LANES]
                tab_ref[entry, 2 * i + 1, at, :] = wide_s[i * LANES : (i + 1) * LANES]
    copies[4].wait()
    high, low = halves(sw_in[...])
    sw_ref[...] = jnp.concatenate([high, low], 1)
    for copy in copies[1:4]:
        copy.wait()


def prologue(levels, sub_count, x, vel, switch):
    tgt = x.shape[1]
    mats = [jnp.asarray(child_matrices(e)) for e in (0, 1)]
    anywhere = pl.BlockSpec(memory_space=pltpu.HBM)
    vmem = pl.BlockSpec(memory_space=pltpu.VMEM)
    return pl.pallas_call(
        functools.partial(prologue_kernel, levels, sub_count),
        out_shape=[
            jax.ShapeDtypeStruct(x.shape, jnp.float32),
            jax.ShapeDtypeStruct(mats[0].shape, jnp.bfloat16),
            jax.ShapeDtypeStruct(mats[1].shape, jnp.bfloat16),
            jax.ShapeDtypeStruct((VEC, 2 * VEC), jnp.bfloat16),
            jax.ShapeDtypeStruct((levels + 1, ENTRIES, tgt, VEC), jnp.float32),
        ],
        in_specs=[anywhere] * 5,
        out_specs=[vmem] * 5,
        scratch_shapes=[
            pltpu.VMEM(vel.shape, jnp.float32),
            pltpu.VMEM(switch.shape, jnp.float32),
            pltpu.SemaphoreType.DMA((5,)),
        ],
        compiler_params=pltpu.CompilerParams(vmem_limit_bytes=VMEM_ROOM),
        name="prologue",
    )(*[pltpu.with_memory_space_constraint(v, pltpu.HBM) for v in (x, vel, mats[0], mats[1], switch)])


def turn(v, c, s):
    return v * c[None] + pltpu.roll(v, POINTS, 2) * s[None]


def bit_of(sub_count, level):
    return ((lax.axis_index("box") * sub_count + lax.axis_index("sub")) // 2**level) % 2


def merged(own, far, tab_ref, entry, start, mat):
    shape = far.shape
    at = slice(start, start + shape[1])
    own = turn(own, tab_ref[entry, 0, at], tab_ref[entry, 1, at])
    far = turn(far, tab_ref[entry, 2, at], tab_ref[entry, 3, at])
    both = jnp.concatenate([own.reshape(-1, VEC), far.reshape(-1, VEC)], 1)
    mixed = mixed_with(both, mat).reshape(shape)
    return turn(mixed, tab_ref[entry, 4, at], tab_ref[entry, 5, at])


def level_value(plan, level, start, own, far, tab_ref, mat_ref, sw_ref):
    result = merged(own, far, tab_ref, level, start, mat_ref[bit_of(plan.sub_count, level)])
    if level == plan.switch_level:
        result = mixed_with(result.reshape(-1, VEC), sw_ref[...]).reshape(result.shape)
    return result


def call(kernel, args, outs, scratch=(), specs=None, out_specs=None, aliases=None):
    specs = list(specs or [VMEM_SPEC] * len(args))
    return pl.pallas_call(
        kernel,
        out_shape=[jax.ShapeDtypeStruct(s, jnp.float32) for s in outs],
        in_specs=specs,
        out_specs=out_specs or [VMEM_SPEC] * len(outs),
        scratch_shapes=list(scratch),
        input_output_aliases=aliases or {},
        compiler_params=pltpu.CompilerParams(vmem_limit_bytes=VMEM_ROOM),
    )(*args)


VMEM_SPEC = pl.BlockSpec(memory_space=pltpu.VMEM)
HBM_SPEC = pl.BlockSpec(memory_space=pltpu.HBM)


class Plan:
    def __init__(self, sub_count, levels, shape):
        self.sub_count = sub_count
        self.sub_bits = sub_count.bit_length() - 1
        self.levels = levels
        self.switch_level = levels // 2 - 1
        self.src, self.tgt, _ = shape
        total = sum(SHARES)
        self.widths = [self.tgt * n // total for n in SHARES]
        self.starts = [sum(self.widths[:c]) for c in range(len(SHARES))]

    def far_of(self, value, level):
        if level < self.sub_bits:
            return swapped(value, "sub", level)
        return swapped(value, "box", level - self.sub_bits)


def first_step(plan, x, far, tab, mat, sw):
    half = plan.src // 2

    def kernel(x_ref, far_ref, tab_ref, mat_ref, sw_ref, *outs):
        result = level_value(plan, 0, 0, x_ref[...], far_ref[...], tab_ref, mat_ref, sw_ref)
        upper = bit_of(plan.sub_count, plan.levels - 1) == 1
        outs = list(outs)
        for start, width, kind in zip(plan.starts, plan.widths, KIND):
            part = result[:, start : start + width]
            if kind == SPLIT:
                outs.pop(0)[...] = jnp.where(upper, part[half:], part[:half])
                outs.pop(0)[...] = jnp.where(upper, part[:half], part[half:])
            else:
                outs.pop(0)[...] = part

    outs = []
    for width, kind in zip(plan.widths, KIND):
        outs += [(half, width, VEC)] * 2 if kind == SPLIT else [(plan.src, width, VEC)]
    outs = list(call(kernel, [x, far, tab, mat, sw], outs))
    return [(outs.pop(0), outs.pop(0)) if kind == SPLIT else (outs.pop(0),) for kind in KIND]


def step(plan, level, c, own, far, tab, mat, sw):
    def kernel(own_ref, far_ref, tab_ref, mat_ref, sw_ref, *rest):
        rest[-1][...] = level_value(plan, level, plan.starts[c], own_ref[...], far_ref[...], tab_ref, mat_ref, sw_ref)

    return call(kernel, [own, far, tab, mat, sw], [own.shape])[0]


def join(kept, received):
    def kernel(a_ref, b_ref, *rest):
        n = a_ref.shape[0]
        rest[-1][:n] = a_ref[...]
        rest[-1][n:] = b_ref[...]

    return call(kernel, [kept, received], [(2 * kept.shape[0], *kept.shape[1:])])[0]


def early_end(plan, c, own, far, tab, mats, sw):
    last = plan.levels - 1
    start = plan.starts[c]

    def kernel(own_ref, far_ref, tab_ref, mat_ref, last_mat_ref, sw_ref, mine_ref, *theirs):
        x = level_value(plan, last - 1, start, own_ref[...], far_ref[...], tab_ref, mat_ref, sw_ref)
        half = x.shape[0] // 2
        mat = last_mat_ref[bit_of(plan.sub_count, last)]
        for ref in theirs:
            ref[...] = merged(x[:half], x[half:], tab_ref, last + 1, start, mat)
        mine_ref[...] = merged(x[:half], x[half:], tab_ref, last, start, mat)

    shape = (own.shape[0] // 2, *own.shape[1:])
    return call(kernel, [own, far, tab, mats[(last - 1) % 2], mats[last % 2], sw], [shape] * (1 + (KIND[c] == SPLIT)))


def finish(plan, results):
    flat = [part for result in results for part in result]

    def kernel(*refs):
        parts, out_hbm, sems = list(refs[: len(flat)]), refs[-2], refs[-1]
        upper = bit_of(plan.sub_count, plan.levels - 1)
        copies = []
        for start, result in zip(plan.starts, results):
            for i in range(len(result)):
                ref = parts.pop(0)
                rows, count, _ = ref.shape
                box = 0 if len(result) == 1 else (upper if i == 0 else 1 - upper) * rows
                place = out_hbm.at[pl.ds(box, rows), pl.ds(start, count)]
                copies.append(pltpu.make_async_copy(ref, place, sems.at[len(copies)]))
        for copy in copies:
            copy.start()
        for copy in copies:
            copy.wait()

    scratch = [pltpu.SemaphoreType.DMA((len(flat),))]
    return call(kernel, flat, [(plan.src, plan.tgt, VEC)], scratch, None, [HBM_SPEC])[0]


def swapped(value, axis, apart):
    mask = 2**apart
    pairs = [(source, source ^ mask) for source in range(lax.axis_size(axis))]
    return lax.ppermute(value, axis, pairs)


def levels_of(box_weights, velocity, switch_kernel):
    sub_count = lax.axis_size("sub")
    levels = lax.axis_size("box").bit_length() - 1 + sub_count.bit_length() - 1
    plan = Plan(sub_count, levels, box_weights.shape)
    last = levels - 1

    far = plan.far_of(box_weights, 0)
    x, even, odd, sw, tab = prologue(levels, sub_count, box_weights, velocity.reshape(-1, LANES), switch_kernel)
    mats = (even, odd)
    parts = first_step(plan, x, far, tab, mats[0], sw)
    results = []
    for c, (part, *leaving) in enumerate(parts):
        if KIND[c] != PLAIN:
            received = plan.far_of((leaving or [part])[0], last)
            part = join(part, received)
        for level in range(1, levels if KIND[c] == PLAIN else last - 1):
            far = plan.far_of(part, level)
            part = step(plan, level, c, part, far, tab, mats[level % 2], sw)
        if KIND[c] == PLAIN:
            results.append((part,))
            continue
        far = plan.far_of(part, last - 1)
        mine, *theirs = early_end(plan, c, part, far, tab, mats, sw)
        results.append((mine, *[plan.far_of(sent, last) for sent in theirs]))
    return finish(plan, results)


def solution(mesh):
    return jax.shard_map(
        levels_of,
        mesh=mesh,
        in_specs=(P(("shot", "box", "sub"), None, None), P("shot"), P()),
        out_specs=P("shot", ("box", "sub"), None),
        check_vma=False,
    )
```

```python
import functools

import jax
import jax.numpy as jnp
import numpy as np
from jax import lax
from jax.experimental import pallas as pl
from jax.experimental.pallas import tpu as pltpu
from jax.sharding import PartitionSpec as P


CHEB = 8
POINTS = CHEB * CHEB
VEC = 2 * POINTS
HALF_ROOT = 0.7071067811865476
SHARES = (14, 9, 9)
PLAIN, SPLIT, DOUBLE = range(3)
KIND = (PLAIN, PLAIN, DOUBLE)
PENDING = 1
LANES = 128
ENTRIES = 6
VMEM_ROOM = 8 << 20


COS_SERIES = [-1.0 / 87178291200.0, 1.0 / 479001600.0, -1.0 / 3628800.0, 1.0 / 40320.0, -1.0 / 720.0, 1.0 / 24.0, -0.5, 1.0]
SIN_SERIES = [-1.0 / 1307674368000.0, 1.0 / 6227020800.0, -1.0 / 39916800.0, 1.0 / 362880.0, -1.0 / 5040.0, 1.0 / 120.0, -1.0 / 6.0, 1.0]


def nodes():
    return np.cos(np.pi * (2.0 * np.arange(CHEB) + 1.0) / (2.0 * CHEB))


def child_matrices(axis_dim):
    z = nodes()
    found = []
    for child in (0, 1):
        y = (z + (2.0 * child - 1.0)) * 0.5
        rows = np.ones((CHEB, CHEB))
        for k in range(CHEB):
            for other in range(CHEB):
                if other != k:
                    rows[:, k] *= (y - z[other]) / (z[k] - z[other])
        single = np.kron(rows, np.eye(CHEB)) if axis_dim == 0 else np.kron(np.eye(CHEB), rows)
        found.append(np.kron(np.eye(2), single).astype(np.float32))
    both = np.stack([np.concatenate(found, 0), np.concatenate(found[::-1], 0)])
    high = both.astype(jnp.bfloat16)
    low = (both - high.astype(np.float32)).astype(jnp.bfloat16)
    return np.concatenate([high, low], -1)


def cos_sin(angle):
    square = angle * angle
    c = jnp.full_like(square, COS_SERIES[0])
    for term in COS_SERIES[1:]:
        c = c * square + term
    s = jnp.full_like(square, SIN_SERIES[0])
    for term in SIN_SERIES[1:]:
        s = s * square + term
    return c, s * angle


def halves(x):
    high = x.astype(jnp.bfloat16)
    return high, (x - high.astype(jnp.float32)).astype(jnp.bfloat16)


def mm(a, b):
    return jnp.dot(a, b, preferred_element_type=jnp.float32)


def mixed_with(x, mat):
    high, low = halves(x)
    m, n = x.shape[0], mat.shape[1] // 2
    wide = mm(jnp.concatenate([high, low], 0), mat)
    return (wide[:m, :n] + wide[m:, :n]) + (wide[:m, n:] + wide[m:, n:])


def expand(values, spots):
    a = values.astype(jnp.bfloat16)
    rest = values - a.astype(jnp.float32)
    b = rest.astype(jnp.bfloat16)
    c = (rest - b.astype(jnp.float32)).astype(jnp.bfloat16)
    pieces = jnp.concatenate([a.astype(jnp.float32), b.astype(jnp.float32), c.astype(jnp.float32)], 0)
    return lax.dot_general(
        pieces.astype(jnp.bfloat16), spots, (((0,), (0,)), ((), ())), preferred_element_type=jnp.float32
    )


def prologue_kernel(levels, sub_count, x_hbm, vel_hbm, even_hbm, odd_hbm, sw_hbm, x_ref, even_ref, odd_ref, sw_ref, tab_ref, vel_ref, sw_in, sems):
    copies = [
        pltpu.make_async_copy(vel_hbm, vel_ref, sems.at[0]),
        pltpu.make_async_copy(x_hbm, x_ref, sems.at[1]),
        pltpu.make_async_copy(even_hbm, even_ref, sems.at[2]),
        pltpu.make_async_copy(odd_hbm, odd_ref, sems.at[3]),
        pltpu.make_async_copy(sw_hbm, sw_in, sems.at[4]),
    ]
    for copy in copies:
        copy.start()
    device = lax.axis_index("box") * sub_count + lax.axis_index("sub")
    tgt = tab_ref.shape[2]
    rows = tgt // LANES
    node = lax.broadcasted_iota(jnp.int32, (CHEB, LANES), 0)
    z = jnp.zeros((CHEB, LANES), jnp.float32)
    for k, value in enumerate(nodes()):
        z = jnp.where(node == k, float(value), z)
    node = lax.broadcasted_iota(jnp.int32, (3 * CHEB, VEC), 0) % CHEB
    lane = lax.broadcasted_iota(jnp.int32, (3 * CHEB, VEC), 1)
    sign = jnp.where(lane < POINTS, -1.0, 1.0)
    point = lane % POINTS
    spots = []
    for spot in (point // CHEB, point % CHEB):
        hit = jnp.where(spot == node, 1.0, 0.0)
        spots.append((hit.astype(jnp.bfloat16), (hit * sign).astype(jnp.bfloat16)))
    copies[0].wait()
    for entry in range(tab_ref.shape[0]):
        level = min(entry, levels - 1)
        code = device % 2 ** (level + 1)
        child = (device // 2**level) % 2
        if entry == levels:
            code = code + (1 - 2 * child) * 2**level
        k = 2.0 * child.astype(jnp.float32) - 1.0
        plain, signed = spots[level % 2]
        for r in range(rows):
            half = 0.5 * jnp.broadcast_to(vel_ref[pl.ds(code * rows + r, 1), :], (CHEB, LANES))
            c1, s1 = cos_sin(half * z)
            ca, sa = cos_sin(half)
            sa = sa * k
            p, q, u, t = c1 * ca, s1 * sa, s1 * ca, c1 * sa
            cosines = (p - q, p + q, (1.0 - 2.0 * s1 * s1) * HALF_ROOT)
            sines = (-(u + t), t - u, (2.0 * HALF_ROOT) * s1 * c1)
            at = slice(r * LANES, (r + 1) * LANES)
            wide = expand(jnp.concatenate(cosines, 1), plain)
            wide_s = expand(jnp.concatenate(sines, 1), signed)
            for i in range(3):
                tab_ref[entry, 2 * i, at, :] = wide[i * LANES : (i + 1) * LANES]
                tab_ref[entry, 2 * i + 1, at, :] = wide_s[i * LANES : (i + 1) * LANES]
    copies[4].wait()
    high, low = halves(sw_in[...])
    sw_ref[...] = jnp.concatenate([high, low], 1)
    for copy in copies[1:4]:
        copy.wait()


def prologue(levels, sub_count, x, vel, switch):
    tgt = x.shape[1]
    mats = [jnp.asarray(child_matrices(e)) for e in (0, 1)]
    anywhere = pl.BlockSpec(memory_space=pltpu.HBM)
    vmem = pl.BlockSpec(memory_space=pltpu.VMEM)
    return pl.pallas_call(
        functools.partial(prologue_kernel, levels, sub_count),
        out_shape=[
            jax.ShapeDtypeStruct(x.shape, jnp.float32),
            jax.ShapeDtypeStruct(mats[0].shape, jnp.bfloat16),
            jax.ShapeDtypeStruct(mats[1].shape, jnp.bfloat16),
            jax.ShapeDtypeStruct((VEC, 2 * VEC), jnp.bfloat16),
            jax.ShapeDtypeStruct((levels + (SPLIT in KIND), ENTRIES, tgt, VEC), jnp.float32),
        ],
        in_specs=[anywhere] * 5,
        out_specs=[vmem] * 5,
        scratch_shapes=[
            pltpu.VMEM(vel.shape, jnp.float32),
            pltpu.VMEM(switch.shape, jnp.float32),
            pltpu.SemaphoreType.DMA((5,)),
        ],
        compiler_params=pltpu.CompilerParams(vmem_limit_bytes=VMEM_ROOM),
        name="prologue",
    )(*[pltpu.with_memory_space_constraint(v, pltpu.HBM) for v in (x, vel, mats[0], mats[1], switch)])


def turn(v, c, s):
    return v * c[None] + pltpu.roll(v, POINTS, 2) * s[None]


def bit_of(sub_count, level):
    return ((lax.axis_index("box") * sub_count + lax.axis_index("sub")) // 2**level) % 2


def merged(own, far, tab_ref, entry, start, mat):
    shape = far.shape
    at = slice(start, start + shape[1])
    own = turn(own, tab_ref[entry, 0, at], tab_ref[entry, 1, at])
    far = turn(far, tab_ref[entry, 2, at], tab_ref[entry, 3, at])
    both = jnp.concatenate([own.reshape(-1, VEC), far.reshape(-1, VEC)], 1)
    mixed = mixed_with(both, mat).reshape(shape)
    return turn(mixed, tab_ref[entry, 4, at], tab_ref[entry, 5, at])


def level_value(plan, level, start, own, far, tab_ref, mat_ref, sw_ref):
    result = merged(own, far, tab_ref, level, start, mat_ref[bit_of(plan.sub_count, level)])
    if level == plan.switch_level:
        result = mixed_with(result.reshape(-1, VEC), sw_ref[...]).reshape(result.shape)
    return result


def call(kernel, args, outs, scratch=(), specs=None, out_specs=None, aliases=None):
    specs = list(specs or [VMEM_SPEC] * len(args))
    return pl.pallas_call(
        kernel,
        out_shape=[jax.ShapeDtypeStruct(s, jnp.float32) for s in outs],
        in_specs=specs,
        out_specs=out_specs or [VMEM_SPEC] * len(outs),
        scratch_shapes=list(scratch),
        input_output_aliases=aliases or {},
        compiler_params=pltpu.CompilerParams(vmem_limit_bytes=VMEM_ROOM),
    )(*args)


VMEM_SPEC = pl.BlockSpec(memory_space=pltpu.VMEM)
HBM_SPEC = pl.BlockSpec(memory_space=pltpu.HBM)


class Plan:
    def __init__(self, sub_count, levels, shape):
        self.sub_count = sub_count
        self.sub_bits = sub_count.bit_length() - 1
        self.levels = levels
        self.switch_level = levels // 2 - 1
        self.src, self.tgt, _ = shape
        total = sum(SHARES)
        self.widths = [self.tgt * n // total for n in SHARES[:-1]]
        self.widths.append(self.tgt - sum(self.widths))
        self.starts = [sum(self.widths[:c]) for c in range(len(SHARES))]

    def far_of(self, value, level):
        if level < self.sub_bits:
            return swapped(value, "sub", level)
        return swapped(value, "box", level - self.sub_bits)


def first_step(plan, x, far, tab, mat, sw):
    half = plan.src // 2

    def kernel(x_ref, far_ref, tab_ref, mat_ref, sw_ref, *outs):
        result = level_value(plan, 0, 0, x_ref[...], far_ref[...], tab_ref, mat_ref, sw_ref)
        upper = bit_of(plan.sub_count, plan.levels - 1) == 1
        outs = list(outs)
        for start, width, kind in zip(plan.starts, plan.widths, KIND):
            part = result[:, start : start + width]
            if kind == SPLIT:
                outs.pop(0)[...] = jnp.where(upper, part[half:], part[:half])
                outs.pop(0)[...] = jnp.where(upper, part[:half], part[half:])
            else:
                outs.pop(0)[...] = part

    outs = []
    for width, kind in zip(plan.widths, KIND):
        outs += [(half, width, VEC)] * 2 if kind == SPLIT else [(plan.src, width, VEC)]
    outs = list(call(kernel, [x, far, tab, mat, sw], outs))
    return [(outs.pop(0), outs.pop(0)) if kind == SPLIT else (outs.pop(0),) for kind in KIND]


def step(plan, level, c, own, far, tab, mat, sw):
    def kernel(own_ref, far_ref, tab_ref, mat_ref, sw_ref, *rest):
        rest[-1][...] = level_value(plan, level, plan.starts[c], own_ref[...], far_ref[...], tab_ref, mat_ref, sw_ref)

    return call(kernel, [own, far, tab, mat, sw], [own.shape])[0]


def join(kept, received):
    def kernel(a_ref, b_ref, *rest):
        n = a_ref.shape[0]
        rest[-1][:n] = a_ref[...]
        rest[-1][n:] = b_ref[...]

    return call(kernel, [kept, received], [(2 * kept.shape[0], *kept.shape[1:])])[0]


def both_levels(plan, c, mine_ref, theirs, own_ref, far_ref, tab_ref, mat_ref, last_mat_ref, sw_ref):
    last = plan.levels - 1
    start = plan.starts[c]
    x = level_value(plan, last - 1, start, own_ref[...], far_ref[...], tab_ref, mat_ref, sw_ref)
    half = x.shape[0] // 2
    mat = last_mat_ref[bit_of(plan.sub_count, last)]
    for ref in theirs:
        ref[...] = merged(x[:half], x[half:], tab_ref, last + 1, start, mat)
    mine_ref[...] = merged(x[:half], x[half:], tab_ref, last, start, mat)


def early_end(plan, c, own, *args):
    def kernel(*refs):
        both_levels(plan, c, refs[len(args) + 1], refs[len(args) + 2 :], *refs[: len(args) + 1])

    shape = (own.shape[0] // 2, *own.shape[1:])
    return call(kernel, [own, *args], [shape] * (1 + (KIND[c] == SPLIT)))


def finish(plan, results, pending):
    flat = [part for result in results for part in result or ()]
    args = list(flat)
    if pending is not None:
        c, *more = pending
        args += more
    scratch = [pltpu.SemaphoreType.DMA((len(flat) + 1,))]
    if pending is not None:
        shape = (plan.src, plan.widths[c], VEC)
        scratch.append(pltpu.VMEM(shape, jnp.float32))

    def kernel(*refs):
        parts, out_hbm, sems = list(refs[: len(flat)]), refs[len(args)], refs[len(args) + 1]
        upper = bit_of(plan.sub_count, plan.levels - 1)
        copies = []
        for start, result in zip(plan.starts, results):
            for i in range(len(result or ())):
                ref = parts.pop(0)
                rows, count, _ = ref.shape
                box = 0 if len(result) == 1 else (upper if i == 0 else 1 - upper) * rows
                place = out_hbm.at[pl.ds(box, rows), pl.ds(start, count)]
                copies.append(pltpu.make_async_copy(ref, place, sems.at[len(copies)]))
        for copy in copies:
            copy.start()
        if pending is not None:
            held = refs[-1]
            own_ref, far_ref, *others = refs[len(flat) : len(args)]
            held[...] = level_value(plan, plan.levels - 1, plan.starts[c], own_ref[...], far_ref[...], *others)
            place = out_hbm.at[:, pl.ds(plan.starts[c], plan.widths[c])]
            copies.append(pltpu.make_async_copy(held, place, sems.at[len(copies)]))
            copies[-1].start()
        for copy in copies:
            copy.wait()

    return call(kernel, args, [(plan.src, plan.tgt, VEC)], scratch, None, [HBM_SPEC])[0]


def swapped(value, axis, apart):
    mask = 2**apart
    pairs = [(source, source ^ mask) for source in range(lax.axis_size(axis))]
    return lax.ppermute(value, axis, pairs)


def levels_of(box_weights, velocity, switch_kernel):
    sub_count = lax.axis_size("sub")
    levels = lax.axis_size("box").bit_length() - 1 + sub_count.bit_length() - 1
    plan = Plan(sub_count, levels, box_weights.shape)
    last = levels - 1

    far = plan.far_of(box_weights, 0)
    x, even, odd, sw, tab = prologue(levels, sub_count, box_weights, velocity.reshape(-1, LANES), switch_kernel)
    mats = (even, odd)
    parts = first_step(plan, x, far, tab, mats[0], sw)
    results, pending = [], None
    for c, (part, *leaving) in enumerate(parts):
        if KIND[c] != PLAIN:
            received = plan.far_of((leaving or [part])[0], last)
            part = join(part, received)
        for level in range(1, levels if KIND[c] == PLAIN else last - 1):
            far = plan.far_of(part, level)
            if level == last and c == PENDING:
                pending = (c, part, far, tab, mats[last % 2], sw)
                break
            part = step(plan, level, c, part, far, tab, mats[level % 2], sw)
        if KIND[c] == PLAIN:
            results.append(None if c == PENDING else (part,))
            continue
        far = plan.far_of(part, last - 1)
        args = (part, far, tab, mats[(last - 1) % 2], mats[last % 2], sw)
        mine, *theirs = early_end(plan, c, *args)
        results.append((mine, *[plan.far_of(sent, last) for sent in theirs]))
    return finish(plan, results, pending)


def solution(mesh):
    return jax.shard_map(
        levels_of,
        mesh=mesh,
        in_specs=(P(("shot", "box", "sub"), None, None), P("shot"), P()),
        out_specs=P("shot", ("box", "sub"), None),
        check_vma=False,
    )
```

```python
import functools

import jax
import jax.numpy as jnp
import numpy as np
from jax import lax
from jax.experimental import pallas as pl
from jax.experimental.pallas import tpu as pltpu
from jax.sharding import PartitionSpec as P


CHEB = 8
POINTS = CHEB * CHEB
VEC = 2 * POINTS
HALF_ROOT = 0.7071067811865476
SHARES = (14, 9, 9)
PLAIN, SPLIT, DOUBLE = range(3)
KIND = (PLAIN, PLAIN, DOUBLE)
PENDING = 1
LANES = 128
ENTRIES = 6
VMEM_ROOM = 8 << 20


COS_SERIES = [-1.0 / 87178291200.0, 1.0 / 479001600.0, -1.0 / 3628800.0, 1.0 / 40320.0, -1.0 / 720.0, 1.0 / 24.0, -0.5, 1.0]
SIN_SERIES = [-1.0 / 1307674368000.0, 1.0 / 6227020800.0, -1.0 / 39916800.0, 1.0 / 362880.0, -1.0 / 5040.0, 1.0 / 120.0, -1.0 / 6.0, 1.0]


def nodes():
    return np.cos(np.pi * (2.0 * np.arange(CHEB) + 1.0) / (2.0 * CHEB))


def child_matrices(axis_dim):
    z = nodes()
    found = []
    for child in (0, 1):
        y = (z + (2.0 * child - 1.0)) * 0.5
        rows = np.ones((CHEB, CHEB))
        for k in range(CHEB):
            for other in range(CHEB):
                if other != k:
                    rows[:, k] *= (y - z[other]) / (z[k] - z[other])
        single = np.kron(rows, np.eye(CHEB)) if axis_dim == 0 else np.kron(np.eye(CHEB), rows)
        found.append(np.kron(np.eye(2), single).astype(np.float32))
    both = np.stack([np.concatenate(found, 0), np.concatenate(found[::-1], 0)])
    high = both.astype(jnp.bfloat16)
    low = (both - high.astype(np.float32)).astype(jnp.bfloat16)
    return np.concatenate([high, low], -1)


def cos_sin(angle):
    square = angle * angle
    c = jnp.full_like(square, COS_SERIES[0])
    for term in COS_SERIES[1:]:
        c = c * square + term
    s = jnp.full_like(square, SIN_SERIES[0])
    for term in SIN_SERIES[1:]:
        s = s * square + term
    return c, s * angle


def halves(x):
    high = x.astype(jnp.bfloat16)
    return high, (x - high.astype(jnp.float32)).astype(jnp.bfloat16)


def mm(a, b):
    return jnp.dot(a, b, preferred_element_type=jnp.float32)


def mixed_with(x, mat):
    high, low = halves(x)
    n = mat.shape[1] // 2
    wide = mm(high, mat)
    return wide[:, :n] + wide[:, n:] + mm(low, mat[:, :n])


def expand(values, spots):
    a = values.astype(jnp.bfloat16)
    rest = values - a.astype(jnp.float32)
    b = rest.astype(jnp.bfloat16)
    c = (rest - b.astype(jnp.float32)).astype(jnp.bfloat16)
    pieces = jnp.concatenate([a.astype(jnp.float32), b.astype(jnp.float32), c.astype(jnp.float32)], 0)
    return lax.dot_general(
        pieces.astype(jnp.bfloat16), spots, (((0,), (0,)), ((), ())), preferred_element_type=jnp.float32
    )


def prologue_kernel(levels, sub_count, x_hbm, vel_hbm, even_hbm, odd_hbm, sw_hbm, x_ref, even_ref, odd_ref, sw_ref, tab_ref, vel_ref, sw_in, sems):
    copies = [
        pltpu.make_async_copy(vel_hbm, vel_ref, sems.at[0]),
        pltpu.make_async_copy(x_hbm, x_ref, sems.at[1]),
        pltpu.make_async_copy(even_hbm, even_ref, sems.at[2]),
        pltpu.make_async_copy(odd_hbm, odd_ref, sems.at[3]),
        pltpu.make_async_copy(sw_hbm, sw_in, sems.at[4]),
    ]
    for copy in copies:
        copy.start()
    device = lax.axis_index("box") * sub_count + lax.axis_index("sub")
    tgt = tab_ref.shape[2]
    rows = tgt // LANES
    node = lax.broadcasted_iota(jnp.int32, (CHEB, LANES), 0)
    z = jnp.zeros((CHEB, LANES), jnp.float32)
    for k, value in enumerate(nodes()):
        z = jnp.where(node == k, float(value), z)
    node = lax.broadcasted_iota(jnp.int32, (3 * CHEB, VEC), 0) % CHEB
    lane = lax.broadcasted_iota(jnp.int32, (3 * CHEB, VEC), 1)
    sign = jnp.where(lane < POINTS, -1.0, 1.0)
    point = lane % POINTS
    spots = []
    for spot in (point // CHEB, point % CHEB):
        hit = jnp.where(spot == node, 1.0, 0.0)
        spots.append((hit.astype(jnp.bfloat16), (hit * sign).astype(jnp.bfloat16)))
    copies[0].wait()
    for entry in range(tab_ref.shape[0]):
        level = min(entry, levels - 1)
        code = device % 2 ** (level + 1)
        child = (device // 2**level) % 2
        if entry == levels:
            code = code + (1 - 2 * child) * 2**level
        k = 2.0 * child.astype(jnp.float32) - 1.0
        plain, signed = spots[level % 2]
        for r in range(rows):
            half = 0.5 * jnp.broadcast_to(vel_ref[pl.ds(code * rows + r, 1), :], (CHEB, LANES))
            c1, s1 = cos_sin(half * z)
            ca, sa = cos_sin(half)
            sa = sa * k
            p, q, u, t = c1 * ca, s1 * sa, s1 * ca, c1 * sa
            cosines = (p - q, p + q, (1.0 - 2.0 * s1 * s1) * HALF_ROOT)
            sines = (-(u + t), t - u, (2.0 * HALF_ROOT) * s1 * c1)
            at = slice(r * LANES, (r + 1) * LANES)
            wide = expand(jnp.concatenate(cosines, 1), plain)
            wide_s = expand(jnp.concatenate(sines, 1), signed)
            for i in range(3):
                tab_ref[entry, 2 * i, at, :] = wide[i * LANES : (i + 1) * LANES]
                tab_ref[entry, 2 * i + 1, at, :] = wide_s[i * LANES : (i + 1) * LANES]
    copies[4].wait()
    high, low = halves(sw_in[...])
    sw_ref[...] = jnp.concatenate([high, low], 1)
    for copy in copies[1:4]:
        copy.wait()


def prologue(levels, sub_count, x, vel, switch):
    tgt = x.shape[1]
    mats = [jnp.asarray(child_matrices(e)) for e in (0, 1)]
    anywhere = pl.BlockSpec(memory_space=pltpu.HBM)
    vmem = pl.BlockSpec(memory_space=pltpu.VMEM)
    return pl.pallas_call(
        functools.partial(prologue_kernel, levels, sub_count),
        out_shape=[
            jax.ShapeDtypeStruct(x.shape, jnp.float32),
            jax.ShapeDtypeStruct(mats[0].shape, jnp.bfloat16),
            jax.ShapeDtypeStruct(mats[1].shape, jnp.bfloat16),
            jax.ShapeDtypeStruct((VEC, 2 * VEC), jnp.bfloat16),
            jax.ShapeDtypeStruct((levels + (SPLIT in KIND), ENTRIES, tgt, VEC), jnp.float32),
        ],
        in_specs=[anywhere] * 5,
        out_specs=[vmem] * 5,
        scratch_shapes=[
            pltpu.VMEM(vel.shape, jnp.float32),
            pltpu.VMEM(switch.shape, jnp.float32),
            pltpu.SemaphoreType.DMA((5,)),
        ],
        compiler_params=pltpu.CompilerParams(vmem_limit_bytes=VMEM_ROOM),
        name="prologue",
    )(*[pltpu.with_memory_space_constraint(v, pltpu.HBM) for v in (x, vel, mats[0], mats[1], switch)])


def turn(v, c, s):
    return v * c[None] + pltpu.roll(v, POINTS, 2) * s[None]


def bit_of(sub_count, level):
    return ((lax.axis_index("box") * sub_count + lax.axis_index("sub")) // 2**level) % 2


def merged(own, far, tab_ref, entry, start, mat):
    shape = far.shape
    at = slice(start, start + shape[1])
    own = turn(own, tab_ref[entry, 0, at], tab_ref[entry, 1, at])
    far = turn(far, tab_ref[entry, 2, at], tab_ref[entry, 3, at])
    both = jnp.concatenate([own.reshape(-1, VEC), far.reshape(-1, VEC)], 1)
    mixed = mixed_with(both, mat).reshape(shape)
    return turn(mixed, tab_ref[entry, 4, at], tab_ref[entry, 5, at])


def level_value(plan, level, start, own, far, tab_ref, mat_ref, sw_ref):
    result = merged(own, far, tab_ref, level, start, mat_ref[bit_of(plan.sub_count, level)])
    if level == plan.switch_level:
        result = mixed_with(result.reshape(-1, VEC), sw_ref[...]).reshape(result.shape)
    return result


def call(kernel, args, outs, scratch=(), specs=None, out_specs=None, aliases=None):
    specs = list(specs or [VMEM_SPEC] * len(args))
    return pl.pallas_call(
        kernel,
        out_shape=[jax.ShapeDtypeStruct(s, jnp.float32) for s in outs],
        in_specs=specs,
        out_specs=out_specs or [VMEM_SPEC] * len(outs),
        scratch_shapes=list(scratch),
        input_output_aliases=aliases or {},
        compiler_params=pltpu.CompilerParams(vmem_limit_bytes=VMEM_ROOM),
    )(*args)


VMEM_SPEC = pl.BlockSpec(memory_space=pltpu.VMEM)
HBM_SPEC = pl.BlockSpec(memory_space=pltpu.HBM)


class Plan:
    def __init__(self, sub_count, levels, shape):
        self.sub_count = sub_count
        self.sub_bits = sub_count.bit_length() - 1
        self.levels = levels
        self.switch_level = levels // 2 - 1
        self.src, self.tgt, _ = shape
        total = sum(SHARES)
        self.widths = [self.tgt * n // total for n in SHARES[:-1]]
        self.widths.append(self.tgt - sum(self.widths))
        self.starts = [sum(self.widths[:c]) for c in range(len(SHARES))]

    def far_of(self, value, level):
        if level < self.sub_bits:
            return swapped(value, "sub", level)
        return swapped(value, "box", level - self.sub_bits)


def first_step(plan, x, far, tab, mat, sw):
    half = plan.src // 2

    def kernel(x_ref, far_ref, tab_ref, mat_ref, sw_ref, *outs):
        result = level_value(plan, 0, 0, x_ref[...], far_ref[...], tab_ref, mat_ref, sw_ref)
        upper = bit_of(plan.sub_count, plan.levels - 1) == 1
        outs = list(outs)
        for start, width, kind in zip(plan.starts, plan.widths, KIND):
            part = result[:, start : start + width]
            if kind == SPLIT:
                outs.pop(0)[...] = jnp.where(upper, part[half:], part[:half])
                outs.pop(0)[...] = jnp.where(upper, part[:half], part[half:])
            else:
                outs.pop(0)[...] = part

    outs = []
    for width, kind in zip(plan.widths, KIND):
        outs += [(half, width, VEC)] * 2 if kind == SPLIT else [(plan.src, width, VEC)]
    outs = list(call(kernel, [x, far, tab, mat, sw], outs))
    return [(outs.pop(0), outs.pop(0)) if kind == SPLIT else (outs.pop(0),) for kind in KIND]


def step(plan, level, c, own, far, tab, mat, sw):
    def kernel(own_ref, far_ref, tab_ref, mat_ref, sw_ref, *rest):
        rest[-1][...] = level_value(plan, level, plan.starts[c], own_ref[...], far_ref[...], tab_ref, mat_ref, sw_ref)

    return call(kernel, [own, far, tab, mat, sw], [own.shape])[0]


def join(kept, received):
    def kernel(a_ref, b_ref, *rest):
        n = a_ref.shape[0]
        rest[-1][:n] = a_ref[...]
        rest[-1][n:] = b_ref[...]

    return call(kernel, [kept, received], [(2 * kept.shape[0], *kept.shape[1:])])[0]


def both_levels(plan, c, mine_ref, theirs, own_ref, far_ref, tab_ref, mat_ref, last_mat_ref, sw_ref):
    last = plan.levels - 1
    start = plan.starts[c]
    x = level_value(plan, last - 1, start, own_ref[...], far_ref[...], tab_ref, mat_ref, sw_ref)
    half = x.shape[0] // 2
    mat = last_mat_ref[bit_of(plan.sub_count, last)]
    for ref in theirs:
        ref[...] = merged(x[:half], x[half:], tab_ref, last + 1, start, mat)
    mine_ref[...] = merged(x[:half], x[half:], tab_ref, last, start, mat)


def early_end(plan, c, own, *args):
    def kernel(*refs):
        both_levels(plan, c, refs[len(args) + 1], refs[len(args) + 2 :], *refs[: len(args) + 1])

    shape = (own.shape[0] // 2, *own.shape[1:])
    return call(kernel, [own, *args], [shape] * (1 + (KIND[c] == SPLIT)))


def finish(plan, results, pending):
    flat = [part for result in results for part in result or ()]
    args = list(flat)
    if pending is not None:
        c, *more = pending
        args += more
    scratch = [pltpu.SemaphoreType.DMA((len(flat) + 1,))]
    if pending is not None:
        shape = (plan.src, plan.widths[c], VEC)
        scratch.append(pltpu.VMEM(shape, jnp.float32))

    def kernel(*refs):
        parts, out_hbm, sems = list(refs[: len(flat)]), refs[len(args)], refs[len(args) + 1]
        upper = bit_of(plan.sub_count, plan.levels - 1)
        copies = []
        for start, result in zip(plan.starts, results):
            for i in range(len(result or ())):
                ref = parts.pop(0)
                rows, count, _ = ref.shape
                box = 0 if len(result) == 1 else (upper if i == 0 else 1 - upper) * rows
                place = out_hbm.at[pl.ds(box, rows), pl.ds(start, count)]
                copies.append(pltpu.make_async_copy(ref, place, sems.at[len(copies)]))
        for copy in copies:
            copy.start()
        if pending is not None:
            held = refs[-1]
            own_ref, far_ref, *others = refs[len(flat) : len(args)]
            held[...] = level_value(plan, plan.levels - 1, plan.starts[c], own_ref[...], far_ref[...], *others)
            place = out_hbm.at[:, pl.ds(plan.starts[c], plan.widths[c])]
            copies.append(pltpu.make_async_copy(held, place, sems.at[len(copies)]))
            copies[-1].start()
        for copy in copies:
            copy.wait()

    return call(kernel, args, [(plan.src, plan.tgt, VEC)], scratch, None, [HBM_SPEC])[0]


def swapped(value, axis, apart):
    mask = 2**apart
    pairs = [(source, source ^ mask) for source in range(lax.axis_size(axis))]
    return lax.ppermute(value, axis, pairs)


def levels_of(box_weights, velocity, switch_kernel):
    sub_count = lax.axis_size("sub")
    levels = lax.axis_size("box").bit_length() - 1 + sub_count.bit_length() - 1
    plan = Plan(sub_count, levels, box_weights.shape)
    last = levels - 1

    far = plan.far_of(box_weights, 0)
    x, even, odd, sw, tab = prologue(levels, sub_count, box_weights, velocity.reshape(-1, LANES), switch_kernel)
    mats = (even, odd)
    parts = first_step(plan, x, far, tab, mats[0], sw)
    results, pending = [], None
    for c, (part, *leaving) in enumerate(parts):
        if KIND[c] != PLAIN:
            received = plan.far_of((leaving or [part])[0], last)
            part = join(part, received)
        for level in range(1, levels if KIND[c] == PLAIN else last - 1):
            far = plan.far_of(part, level)
            if level == last and c == PENDING:
                pending = (c, part, far, tab, mats[last % 2], sw)
                break
            part = step(plan, level, c, part, far, tab, mats[level % 2], sw)
        if KIND[c] == PLAIN:
            results.append(None if c == PENDING else (part,))
            continue
        far = plan.far_of(part, last - 1)
        args = (part, far, tab, mats[(last - 1) % 2], mats[last % 2], sw)
        mine, *theirs = early_end(plan, c, *args)
        results.append((mine, *[plan.far_of(sent, last) for sent in theirs]))
    return finish(plan, results, pending)


def solution(mesh):
    return jax.shard_map(
        levels_of,
        mesh=mesh,
        in_specs=(P(("shot", "box", "sub"), None, None), P("shot"), P()),
        out_specs=P("shot", ("box", "sub"), None),
        check_vma=False,
    )
```
